512 devices in a mesh: segment: 64 (over y, x, z_hi, core), fsdp: 8 (over z_lo).
Axes of the slice: x: 4, y: 4, z: 16 (z_hi: 2, z_lo: 8; z = z_hi * 8 + z_lo), core: 2. Of those that a mesh axis runs over, the one named last changes fastest.
Arguments:
- stream: bfloat16 [2, 64, 512, 4096], P(None, 'segment', 'fsdp'), may hold values from -60 to 60
- gain: bfloat16 [2, 64, 4096], P(None, 'segment'), may hold values from 0.099609375 to 1.8984375
- w_query: bfloat16 [2, 64, 32, 128, 128], P(None, 'segment', 'fsdp'), may hold values from -20 to 20
- w_key: bfloat16 [2, 64, 32, 128, 128], P(None, 'segment', 'fsdp'), may hold values from -20 to 20
- w_value: bfloat16 [2, 64, 32, 128, 128], P(None, 'segment', 'fsdp'), may hold values from -0.5 to 0.5
- w_mix: bfloat16 [2, 64, 128, 32, 32], P(None, 'segment', 'fsdp'), may hold values from -1 to 1
- active: int32 [2, 64], P(None, 'segment'), may hold values from 0 to 1
- random_blocks: int32 [2, 64, 8, 2], P(None, 'segment'), may hold values from 0 to 7
Outputs:
- advanced: bfloat16 [2, 64, 512, 4096], P(None, 'segment', 'fsdp')
The draws below stay inside these ranges and needn't reach their ends.
All inputs are finite; a program needn't handle non-finite values.
Results may differ from the reference program's by a relative error of at most 0.009.
Values may be sent and summed in bfloat16 or wider, within the bound.
No kernel may reach another device: no remote copies, remote signals or barrier semaphores. Data moves between devices by JAX's collectives and lax.ppermute only.
A program may use at most 64 MiB of HBM per device.

```python
import math
import jax
import jax.numpy as jnp
from jax import lax

HEADS = 32
HS = 128
D = 4096
BLK = 64
R = 2
V = 2
ROUNDS = 2
SEQ = 512
NB = 8
N_SEGMENT = 64


def draw_stream(key, part):
    own_key = jax.random.fold_in(key, 101)
    first, second, third = jax.random.split(own_key, 3)
    shape = (V, N_SEGMENT, SEQ, D)
    row_scale = jnp.exp(jax.random.uniform(second, (V, N_SEGMENT, SEQ, 1), jnp.float32, math.log(0.3), math.log(3.0)))
    col_scale = jnp.exp(jax.random.uniform(third, (V, N_SEGMENT, 1, D), jnp.float32, math.log(0.3), math.log(3.0)))
    base = jnp.clip(jax.random.normal(first, shape, jnp.float32), -6.0, 6.0)
    return (base * row_scale * col_scale).astype(jnp.bfloat16)


def draw_w_query(key, part):
    own_key = jax.random.fold_in(key, 202)
    shape = (V, N_SEGMENT, HEADS, HS, HS)
    base = jnp.clip(jax.random.normal(own_key, shape, jnp.float32), -6.0, 6.0) * HS ** (-0.5)
    return base.astype(jnp.bfloat16)


def draw_w_key(key, part):
    own_key = jax.random.fold_in(key, 303)
    shape = (V, N_SEGMENT, HEADS, HS, HS)
    base = jnp.clip(jax.random.normal(own_key, shape, jnp.float32), -6.0, 6.0) * HS ** (-0.5)
    return base.astype(jnp.bfloat16)


def plant(drawn, key, low, top_value):
    shape = drawn.shape
    spot = [jax.random.randint(jax.random.fold_in(key, axis), (), 0, shape[axis]) for axis in range(len(shape))]
    drawn = drawn.at[tuple(spot)].set(low)
    longest = shape.index(max(shape))
    spot[longest] = (spot[longest] + 1) % shape[longest]
    return drawn.at[tuple(spot)].set(top_value)


def shard_levels(key, extent, pieces, least, high):
    level = 1.0
    for dim, blocks in pieces:
        draws = jax.random.uniform(jax.random.fold_in(jax.random.fold_in(key, 6), dim), (blocks,), jnp.float32, least / len(pieces), high / len(pieces))
        level = level * jnp.repeat(jnp.exp(draws), extent[dim] // blocks).reshape((-1,) + (1,) * (len(extent) - 1 - dim))
    return level


def bell_draw(key, shape, deviation, limit, cuts=(), held_as=jnp.bfloat16):
    level = shard_levels(key, shape, cuts, -0.22, 0.18) if cuts else 1.0
    drawn = jax.random.normal(key, shape, jnp.float32) * deviation * level
    return jnp.minimum(jnp.maximum(drawn, -limit), limit).astype(held_as)


def setup_inputs(seed: int = 0) -> dict:
    streams_of = jax.random.split(jax.random.key(seed), 9)
    stream = draw_stream(jax.random.fold_in(streams_of[8], 71), 0)
    gain = jnp.clip(1.0 + 0.18 * jax.random.normal(streams_of[1], (V, N_SEGMENT, D), jnp.float32), 0.099609375, 1.8984375).astype(jnp.bfloat16)
    w_query = draw_w_query(jax.random.fold_in(streams_of[8], 71), 0)
    w_key = draw_w_key(jax.random.fold_in(streams_of[8], 71), 0)
    w_value = bell_draw(streams_of[4], (V, N_SEGMENT, HEADS, HS, HS), HS ** -0.5, 0.5, ((1, 64), (2, 8)))
    w_mix = bell_draw(streams_of[5], (V, N_SEGMENT, HS, HEADS, HEADS), HEADS ** -0.5, 1.0, ((1, 64), (2, 8)))
    active = plant(jax.random.randint(streams_of[6], (V, N_SEGMENT), 0, 2), jax.random.fold_in(streams_of[6], 1), 0, 1).astype(jnp.int32)
    random_blocks = plant(jax.random.randint(streams_of[7], (V, N_SEGMENT, NB, R), 0, NB), jax.random.fold_in(streams_of[7], 1), 0, NB - 1).astype(jnp.int32)
    return {"stream": stream, "gain": gain, "w_query": w_query, "w_key": w_key, "w_value": w_value, "w_mix": w_mix, "active": active, "random_blocks": random_blocks}


EPS = 1e-05

def block_attention(query, keys, values, random_ids):
    count = SEQ // BLK
    query_blocks = query.reshape(count, BLK, HEADS, HS).astype(jnp.float32)
    key_blocks = keys.reshape(count, BLK, HEADS, HS)
    value_blocks = values.reshape(count, BLK, HEADS, HS)
    block_ids = jnp.arange(count, dtype=jnp.int32)
    window = jnp.stack([(block_ids - 1) % count, block_ids, (block_ids + 1) % count, jnp.zeros_like(block_ids)], axis=1)
    chosen = jnp.concatenate([window, random_ids.astype(jnp.int32)], axis=1)
    picked_keys = key_blocks[chosen].reshape(count, chosen.shape[1] * BLK, HEADS, HS).astype(jnp.float32)
    picked_values = value_blocks[chosen].reshape(count, chosen.shape[1] * BLK, HEADS, HS).astype(jnp.float32)
    scores = jnp.einsum('nqhd,nkhd->nhqk', query_blocks, picked_keys)
    row_max = lax.optimization_barrier(jnp.max(scores, axis=-1, keepdims=True))
    powers = jnp.exp(scores - row_max)
    weights = (powers / lax.optimization_barrier(jnp.sum(powers, axis=-1, keepdims=True))).astype(jnp.bfloat16)
    mixed = jnp.einsum('nhqk,nkhd->nqhd', weights.astype(jnp.float32), picked_values).astype(jnp.bfloat16)
    return mixed.reshape(SEQ, HEADS, HS)

def layer(state, gains, queries_w, keys_w, values_w, mix_w, live, random_ids):
    wide = state.astype(jnp.float32)
    mean_sq = lax.optimization_barrier(jnp.mean(wide * wide, axis=1, keepdims=True))
    normed = (wide * lax.rsqrt(mean_sq + EPS) * gains.astype(jnp.float32)).astype(jnp.bfloat16)
    view = normed.reshape(SEQ, HEADS, HS).astype(jnp.float32)
    raw = jnp.einsum('thc,hcd->thd', view, queries_w.astype(jnp.float32))
    query = (raw * HS ** (-0.5)).astype(jnp.bfloat16)
    keys = jnp.einsum('thc,hcd->thd', view, keys_w.astype(jnp.float32)).astype(jnp.bfloat16)
    values = jnp.einsum('thc,hcd->thd', view, values_w.astype(jnp.float32)).astype(jnp.bfloat16)
    attended = block_attention(query, keys, values, random_ids)
    mixed = jnp.einsum('thc,chg->tgc', attended.astype(jnp.float32), mix_w.astype(jnp.float32)).astype(jnp.bfloat16)
    updated = (wide + mixed.reshape(SEQ, D).astype(jnp.float32)).astype(jnp.bfloat16)
    return jnp.where(live > 0, updated, state)

def reference(stream, gain, w_query, w_key, w_value, w_mix, active, random_blocks):
    count = V * N_SEGMENT
    flat = stream.reshape(count, SEQ, D)
    params = (gain.reshape(count, D), w_query.reshape(count, HEADS, HS, HS), w_key.reshape(count, HEADS, HS, HS), w_value.reshape(count, HEADS, HS, HS), w_mix.reshape(count, HS, HEADS, HEADS), active.reshape(count), random_blocks.reshape(count, NB, R))

    def apply_layer(items):
        extra = items[1]
        return layer(items[0], extra[0], extra[1], extra[2], extra[3], extra[4], extra[5], extra[6])
    for round_index in range(ROUNDS):
        flat = jnp.roll(lax.map(apply_layer, (flat, params)), 1, axis=0)
    return flat.reshape(V, N_SEGMENT, SEQ, D)
```

```python
import jax
import jax.numpy as jnp
from jax import lax
from jax.experimental import pallas as pl
from jax.experimental.pallas import tpu as pltpu
from jax.sharding import PartitionSpec as P

BLK = 64
ROUNDS = 2
EPS = 1e-05
BF = jnp.bfloat16
F32 = jnp.float32


def norm_kernel(which, x_ref, gain_ref, out_ref):
    groups, rows, width = out_ref.shape
    for start in range(0, rows, 16):
        wide = x_ref[start : start + 16, :].astype(F32)
        mean_sq = jnp.mean(wide * wide, axis=1, keepdims=True)
        normed = wide * lax.rsqrt(mean_sq + EPS) * gain_ref[0].astype(F32)
        normed = normed.astype(BF)
        for group in range(groups):
            out_ref[group, start : start + 16, :] = normed[:, group * width : (group + 1) * width]


def norm(which, x, gain, groups):
    rows, features = x.shape
    out = jax.ShapeDtypeStruct((groups, rows, features // groups), BF)
    return pl.pallas_call(
        norm_kernel,
        out_shape=out,
        grid_spec=pltpu.PrefetchScalarGridSpec(
            num_scalar_prefetch=1,
            grid=(1,),
            in_specs=[
                pl.BlockSpec((rows, features), lambda i, which: (0, 0)),
                pl.BlockSpec((1, 1, features), lambda i, which: (which[0], 0, 0)),
            ],
            out_specs=pl.BlockSpec(out.shape, lambda i, which: (0, 0, 0)),
        ),
        cost_estimate=pl.CostEstimate(
            flops=rows * features * 6, bytes_accessed=rows * features * 4, transcendentals=rows
        ),
        name="norm",
    )(which, x, gain)


def attention_kernel(which, ids, rows_ref, wq_ref, wk_ref, wv_ref, out_ref, k_ref, v_ref):
    count, block, width = rows_ref.shape
    rows = rows_ref[...].reshape(count * block, width)
    query = jnp.dot(rows, wq_ref[0, 0], preferred_element_type=F32)
    query = (query * width ** (-0.5)).astype(BF)
    k_ref[...] = jnp.dot(rows, wk_ref[0, 0], preferred_element_type=F32).astype(BF)
    v_ref[...] = jnp.dot(rows, wv_ref[0, 0], preferred_element_type=F32).astype(BF)
    picks = ids.shape[0] // (2 * count)
    base = which[0] * count * picks
    for i in range(count):
        starts = [(i - 1) % count * block, i * block, (i + 1) % count * block, 0]
        for r in range(picks):
            starts.append(pl.multiple_of(ids[base + i * picks + r] * block, block))
        keys = jnp.concatenate([k_ref[pl.ds(s, block), :] for s in starts], axis=0)
        values = jnp.concatenate([v_ref[pl.ds(s, block), :] for s in starts], axis=0)
        scores = lax.dot_general(
            query[i * block : (i + 1) * block],
            keys,
            (((1,), (1,)), ((), ())),
            preferred_element_type=F32,
        )
        powers = jnp.exp(scores - jnp.max(scores, axis=1, keepdims=True))
        total = jnp.sum(powers, axis=1, keepdims=True)
        mixed = jnp.dot(powers.astype(BF), values, preferred_element_type=F32)
        out_ref[i] = (mixed / total).astype(BF)


def attention(which, ids, rows, wq, wk, wv):
    count, block, features = rows.shape
    heads, width = wq.shape[1], wq.shape[2]
    weight_spec = pl.BlockSpec((1, 1, width, width), lambda h, which, ids: (which[0], h, 0, 0))
    row_spec = pl.BlockSpec((count, block, width), lambda h, which, ids: (0, 0, h))
    return pl.pallas_call(
        attention_kernel,
        out_shape=jax.ShapeDtypeStruct(rows.shape, BF),
        grid_spec=pltpu.PrefetchScalarGridSpec(
            num_scalar_prefetch=2,
            grid=(heads,),
            in_specs=[row_spec, weight_spec, weight_spec, weight_spec],
            out_specs=row_spec,
            scratch_shapes=[pltpu.VMEM((count * block, width), BF)] * 2,
        ),
        cost_estimate=pl.CostEstimate(
            flops=heads * count * block * width * (6 * width + 4 * 6 * block),
            bytes_accessed=count * block * features * 4 + heads * width * width * 6,
            transcendentals=heads * count * block * 6 * block,
        ),
        name="attention",
    )(which, ids, rows, wq, wk, wv)


def mix_weights_kernel(place, gathered_ref, out_ref):
    groups = gathered_ref.shape[0]
    for v in range(out_ref.shape[0]):
        rows = jnp.concatenate([gathered_ref[place[j], v] for j in range(groups)], axis=0)
        out_ref[v] = rows.astype(F32).T


def gather_mix_weights(w_mix, size):
    me = lax.axis_index("fsdp")
    layers, mine, heads, _ = w_mix.shape
    held = w_mix.reshape(1, layers, mine, heads * heads)
    bits = size.bit_length() - 1
    order = [0]
    for b in reversed(range(bits)):
        other = lax.ppermute(held, "fsdp", [(i, i ^ (1 << b)) for i in range(size)])
        held = jnp.concatenate([held, other], axis=0)
        order = order + [o ^ (1 << b) for o in order]
    back = [0] * size
    for position, o in enumerate(order):
        back[o] = position
    place = jnp.array(back, jnp.int32)[jnp.arange(size, dtype=jnp.int32) ^ me]
    return pl.pallas_call(
        mix_weights_kernel,
        out_shape=jax.ShapeDtypeStruct((layers, heads * heads, mine * size), F32),
        grid_spec=pltpu.PrefetchScalarGridSpec(
            num_scalar_prefetch=1,
            grid=(1,),
            in_specs=[pl.BlockSpec(held.shape, lambda i, place: (0, 0, 0, 0))],
            out_specs=pl.BlockSpec(
                (layers, heads * heads, mine * size), lambda i, place: (0, 0, 0)
            ),
        ),
        name="mix_weights",
    )(place, held)


def mix_kernel(which, active, att_ref, w_ref, x_ref, out_ref, wide_ref):
    groups, rows, features = att_ref.shape
    width = w_ref.shape[2]
    per = features // width
    heads = groups * per
    for h in range(heads):
        lanes = pl.ds(h % per * width, width)
        wide_ref[h] = att_ref[h // per, :, lanes].astype(F32)
    live = active[which[0]] > 0
    step = 4

    def body(i, carry):
        totals = [jnp.zeros((rows, width), F32) for _ in range(step)]
        for h in range(heads):
            attended = wide_ref[h]
            for k in range(step):
                row = w_ref[0, pl.ds(h * heads + i * step + k, 1), :]
                totals[k] = totals[k] + attended * row
        for k in range(step):
            lanes = pl.ds(pl.multiple_of((i * step + k) * width, width), width)
            state = x_ref[:, lanes]
            updated = (state.astype(F32) + totals[k].astype(BF).astype(F32)).astype(BF)
            out_ref[:, lanes] = jnp.where(live, updated, state)
        return carry

    lax.fori_loop(0, heads // step, body, 0)


def mix(which, active, attended, weights, x):
    rows, features = x.shape
    heads2, width = weights.shape[1:]
    return pl.pallas_call(
        mix_kernel,
        out_shape=jax.ShapeDtypeStruct(x.shape, BF),
        grid_spec=pltpu.PrefetchScalarGridSpec(
            num_scalar_prefetch=2,
            grid=(1,),
            in_specs=[
                pl.BlockSpec(attended.shape, lambda i, which, active: (0, 0, 0)),
                pl.BlockSpec((1, heads2, width), lambda i, which, active: (which[0], 0, 0)),
                pl.BlockSpec((rows, features), lambda i, which, active: (0, 0)),
            ],
            out_specs=pl.BlockSpec((rows, features), lambda i, which, active: (0, 0)),
            scratch_shapes=[pltpu.VMEM((features // width, rows, width), F32)],
        ),
        cost_estimate=pl.CostEstimate(
            flops=rows * heads2 * width * 2,
            bytes_accessed=rows * features * 6 + heads2 * width * 4,
            transcendentals=0,
        ),
        name="mix",
    )(which, active, attended, weights, x)


def exchange(value):
    return lax.all_to_all(value, "fsdp", split_axis=0, concat_axis=0, tiled=True)


def shifted(value):
    devices = lax.axis_size("segment")
    return lax.ppermute(value, "segment", [(i, (i + 1) % devices) for i in range(devices)])


def shards(stream, gain, w_query, w_key, w_value, w_mix, active, random_blocks):
    segment = lax.axis_index("segment")
    size = lax.axis_size("fsdp")
    slots = stream.shape[0]
    wq, wk, wv = w_query[:, 0], w_key[:, 0], w_value[:, 0]
    live = active[:, 0]
    ids = random_blocks[:, 0].reshape(-1)
    states = [stream[k, 0] for k in range(slots)]
    mix_w = gather_mix_weights(w_mix[:, 0], size)
    for r in range(ROUNDS):
        for k in range(slots):
            turn = jnp.where(segment < r, 1, 0)
            which = ((k + turn) % slots).astype(jnp.int32).reshape(1)
            rows = exchange(norm(which, states[k], gain, size))
            attended = exchange(attention(which, ids, rows, wq, wk, wv))
            states[k] = shifted(mix(which, live, attended, mix_w, states[k]))
    first = segment < ROUNDS
    outs = [jnp.where(first, states[(k + 1) % slots], states[k]) for k in range(slots)]
    return jnp.stack(outs)[:, None]


def solution(mesh):
    in_specs = (
        P(None, "segment", "fsdp", None),
        P(None, "segment", None),
        P(None, "segment", "fsdp", None, None),
        P(None, "segment", "fsdp", None, None),
        P(None, "segment", "fsdp", None, None),
        P(None, "segment", "fsdp", None, None),
        P(None, "segment"),
        P(None, "segment", None, None),
    )
    out_specs = P(None, "segment", "fsdp", None)
    return jax.shard_map(shards, mesh=mesh, in_specs=in_specs, out_specs=out_specs, check_vma=False)
```

```python
import jax
import jax.numpy as jnp
from jax import lax
from jax.experimental import pallas as pl
from jax.experimental.pallas import tpu as pltpu
from jax.sharding import PartitionSpec as P

BLK = 64
EPS = 1e-05
BF = jnp.bfloat16
F32 = jnp.float32
EARLY = 2


def norm_kernel(which, x_ref, gain_ref, out_ref):
    groups, rows, width = out_ref.shape
    for start in range(0, rows, 16):
        wide = x_ref[start : start + 16, :].astype(F32)
        mean_sq = jnp.mean(wide * wide, axis=1, keepdims=True)
        normed = wide * lax.rsqrt(mean_sq + EPS) * gain_ref[0].astype(F32)
        normed = normed.astype(BF)
        for group in range(groups):
            out_ref[group, start : start + 16, :] = normed[:, group * width : (group + 1) * width]


def norm(which, x, gain, groups):
    slots, rows, features = x.shape
    width = features // groups
    return pl.pallas_call(
        norm_kernel,
        out_shape=jax.ShapeDtypeStruct((groups, slots, rows, width), BF),
        grid_spec=pltpu.PrefetchScalarGridSpec(
            num_scalar_prefetch=1,
            grid=(slots,),
            in_specs=[
                pl.BlockSpec((None, rows, features), lambda k, which: (k, 0, 0)),
                pl.BlockSpec((1, 1, features), lambda k, which: (which[k], 0, 0)),
            ],
            out_specs=pl.BlockSpec((groups, None, rows, width), lambda k, which: (0, k, 0, 0)),
        ),
        cost_estimate=pl.CostEstimate(
            flops=slots * rows * features * 6,
            bytes_accessed=slots * rows * features * 4,
            transcendentals=slots * rows,
        ),
        name="norm",
    )(which, x, gain)


def attend(wq, wk, wv, rows_ref, s_ref, p_ref, block, ids, base):
    keys = s_ref.shape[1]
    width = rows_ref.shape[1]
    count = keys // block
    picks = ids.shape[0] // (2 * count)
    rows = rows_ref[...]
    query = jnp.dot(rows, wq, preferred_element_type=F32)
    query = (query * width ** (-0.5)).astype(BF)
    key = jnp.dot(rows, wk, preferred_element_type=F32).astype(BF)
    value = jnp.dot(rows, wv, preferred_element_type=F32).astype(BF)
    s_ref[...] = lax.dot_general(query, key, (((1,), (1,)), ((), ())), preferred_element_type=F32)
    listed = lax.broadcasted_iota(jnp.int32, (8, keys), 1) // block
    totals = []
    for i in range(count):
        times = jnp.zeros((8, keys), F32)
        near = [(i - 1) % count, i, (i + 1) % count, 0]
        for b in near + [ids[base + i * picks + r] for r in range(picks)]:
            times = times + (listed == b).astype(F32)
        times = times[:1]
        at = slice(i * block, (i + 1) * block)
        scores = jnp.where(times > 0, s_ref[at, :], -jnp.inf)
        powers = jnp.exp(scores - jnp.max(scores, axis=1, keepdims=True)) * times
        totals.append(jnp.sum(powers, axis=1, keepdims=True))
        p_ref[at, :] = powers.astype(BF)
    mixed = jnp.dot(p_ref[...], value, preferred_element_type=F32)
    return (mixed / jnp.concatenate(totals, axis=0)).astype(BF)


def attention_kernel(which, ids, in_ref, wq_ref, wk_ref, wv_ref, out_ref, *scratch):
    rows_ref = scratch[0]
    count, block, width = in_ref.shape
    rows_ref[...] = in_ref[...].reshape(count * block, width)
    base = which[pl.program_id(0)] * (ids.shape[0] // 2)
    mixed = attend(wq_ref[...], wk_ref[...], wv_ref[...], *scratch, block, ids, base)
    out_ref[...] = mixed.reshape(count, block, width)


def attention_scratch(rows, width):
    return [pltpu.VMEM((rows, width), BF), pltpu.VMEM((rows, rows), F32), pltpu.VMEM((rows, rows), BF)]


def attention_cost(slots, heads, count, block, width):
    return pl.CostEstimate(
        flops=slots * heads * count * block * width * (6 * width + 4 * 6 * block),
        bytes_accessed=slots * heads * (count * block * width * 4 + width * width * 6),
        transcendentals=slots * heads * count * block * 6 * block,
    )


def attention(which, ids, rows, wq, wk, wv):
    count, slots, block, features = rows.shape
    heads, width = wq.shape[1], wq.shape[2]
    weight_spec = pl.BlockSpec(
        (None, None, width, width), lambda k, h, which, ids: (which[k], h, 0, 0)
    )
    row_spec = pl.BlockSpec((count, None, block, width), lambda k, h, which, ids: (0, k, 0, h))
    return pl.pallas_call(
        attention_kernel,
        out_shape=jax.ShapeDtypeStruct(rows.shape, BF),
        grid_spec=pltpu.PrefetchScalarGridSpec(
            num_scalar_prefetch=2,
            grid=(slots, heads),
            in_specs=[row_spec, weight_spec, weight_spec, weight_spec],
            out_specs=row_spec,
            scratch_shapes=attention_scratch(count * block, width),
        ),
        cost_estimate=attention_cost(slots, heads, count, block, width),
        name="attention",
    )(which, ids, rows, wq, wk, wv)


def mix_weights_kernel(place, gathered_ref, out_ref):
    groups = gathered_ref.shape[0]
    for v in range(out_ref.shape[0]):
        rows = jnp.concatenate([gathered_ref[place[j], v] for j in range(groups)], axis=0)
        out_ref[v] = rows.astype(F32).T


def partner(value, bit):
    size = lax.axis_size("fsdp")
    other = lax.ppermute(value, "fsdp", [(i, i ^ bit) for i in range(size)])
    return jnp.concatenate([value, other], axis=0)


def gathered_place(bits):
    order = [0]
    for bit in bits:
        order = order + [o ^ bit for o in order]
    back = [0] * len(order)
    for position, o in enumerate(order):
        back[o] = position
    me = lax.axis_index("fsdp")
    return jnp.array(back, jnp.int32)[jnp.arange(len(order), dtype=jnp.int32) ^ me]


def mix_weights(place, held):
    size, layers, mine, pairs = held.shape
    return pl.pallas_call(
        mix_weights_kernel,
        out_shape=jax.ShapeDtypeStruct((layers, pairs, mine * size), F32),
        grid_spec=pltpu.PrefetchScalarGridSpec(
            num_scalar_prefetch=1,
            grid=(1,),
            in_specs=[pl.BlockSpec(held.shape, lambda i, place: (0, 0, 0, 0))],
            out_specs=pl.BlockSpec((layers, pairs, mine * size), lambda i, place: (0, 0, 0)),
        ),
        name="mix_weights",
    )(place, held)


def mix_totals(wide_ref, w_ref, i, step):
    heads, rows, width = wide_ref.shape
    totals = [jnp.zeros((rows, width), F32) for _ in range(step)]
    for h in range(heads):
        attended = wide_ref[h]
        for k in range(step):
            row = w_ref[0, pl.ds(h * heads + i * step + k, 1), :]
            totals[k] = totals[k] + attended * row
    return [total.astype(BF).astype(F32) for total in totals]


def mix_send_kernel(which, me, att_ref, w_ref, x_ref, *refs):
    out_refs, (wide_ref, state_ref) = refs[:-2], refs[-2:]
    groups, rows, features = att_ref.shape
    width = w_ref.shape[2]
    per = features // width
    heads = groups * per
    tile = out_refs[0].shape[1]
    tiles = rows // tile
    for h in range(heads):
        lanes = pl.ds(h % per * width, width)
        wide_ref[h] = att_ref[h // per, :, lanes].astype(F32)
    step = 4

    def body(i, squares):
        totals = mix_totals(wide_ref, w_ref, i, step)
        for k in range(step):
            g = i * step + k
            lanes = pl.ds(pl.multiple_of(g * width, width), width)
            updated = (x_ref[:, lanes].astype(F32) + totals[k]).astype(BF)
            state_ref[g] = updated
            wide = updated.astype(F32)
            squares = squares + wide * wide
        return squares

    squares = lax.fori_loop(0, heads // step, body, jnp.zeros((rows, width), F32))
    mean_sq = jnp.sum(squares, axis=1, keepdims=True) / (heads * width)
    scale = lax.rsqrt(mean_sq + EPS)
    lane = lax.broadcasted_iota(jnp.int32, (tile, width), 1)
    packed = jnp.zeros((tile, width), F32)
    for t in range(tiles):
        rest = scale[t * tile : (t + 1) * tile]
        for term in range(3):
            top = rest.astype(BF).astype(F32)
            packed = jnp.where(lane == t * 4 + term, top, packed)
            rest = rest - top
    packed = packed.astype(BF)
    for r, out_ref in enumerate(out_refs):
        group = me[0] ^ r
        for h in range(per):
            out_ref[h * tiles : (h + 1) * tiles] = state_ref[group * per + h].reshape(
                tiles, tile, width
            )
        out_ref[per * tiles] = packed


def mix_cost(slots, rows, features, pairs, width):
    return pl.CostEstimate(
        flops=slots * rows * pairs * width * 2,
        bytes_accessed=slots * (rows * features * 6 + pairs * width * 4),
        transcendentals=0,
    )


def mix_send(which, me, attended, weights, x):
    slots, rows, features = x.shape
    groups = attended.shape[0]
    pairs, width = weights.shape[1:]
    tile = 16
    share = features // groups
    block = (rows // tile * (share // width) + 1, tile, width)
    heads = features // width
    return pl.pallas_call(
        mix_send_kernel,
        out_shape=[jax.ShapeDtypeStruct((slots, *block), BF)] * groups,
        grid_spec=pltpu.PrefetchScalarGridSpec(
            num_scalar_prefetch=2,
            grid=(slots,),
            in_specs=[
                pl.BlockSpec((groups, None, rows, share), lambda k, which, me: (0, k, 0, 0)),
                pl.BlockSpec((1, pairs, width), lambda k, which, me: (which[k], 0, 0)),
                pl.BlockSpec((None, rows, features), lambda k, which, me: (k, 0, 0)),
            ],
            out_specs=[pl.BlockSpec((None, *block), lambda k, which, me: (k, 0, 0, 0))] * groups,
            scratch_shapes=[
                pltpu.VMEM((heads, rows, width), F32),
                pltpu.VMEM((heads, rows, width), BF),
            ],
        ),
        cost_estimate=mix_cost(slots, rows, features, pairs, width),
        name="mix_send",
    )(which, me, attended, weights, x)


def attention_send_kernel(which, me, ids, *refs):
    size = (len(refs) - 7) // 2
    in_refs, rest = refs[:size], refs[size:]
    gain_ref, wq_ref, wk_ref, wv_ref = rest[:4]
    out_refs, scratch = rest[4:-3], rest[-3:]
    rows_ref = scratch[0]
    slot, head = pl.program_id(0), pl.program_id(1)
    block, width = out_refs[0].shape
    tile = in_refs[0].shape[1]
    tiles = block // tile
    gain = gain_ref[0].astype(F32)
    for k, ref in enumerate(in_refs):
        start = pl.multiple_of((me[0] ^ k) * block, block)
        rows = ref[pl.ds(head * tiles, tiles)].reshape(block, width)
        packed = ref[ref.shape[0] - 1].astype(F32)
        scale = jnp.concatenate(
            [
                packed[:, 4 * t : 4 * t + 1]
                + packed[:, 4 * t + 1 : 4 * t + 2]
                + packed[:, 4 * t + 2 : 4 * t + 3]
                for t in range(tiles)
            ],
            axis=0,
        )
        rows_ref[pl.ds(start, block), :] = (rows.astype(F32) * scale * gain).astype(BF)
    base = which[slot] * (ids.shape[0] // 2)
    mixed = attend(wq_ref[...], wk_ref[...], wv_ref[...], *scratch, block, ids, base)
    rows_ref[...] = mixed
    for k, out_ref in enumerate(out_refs):
        start = pl.multiple_of((me[0] ^ k) * block, block)
        out_ref[...] = rows_ref[pl.ds(start, block), :]


def attention_send(which, me, ids, blocks, gain, wq, wk, wv):
    size = len(blocks)
    slots = blocks[0].shape[0]
    heads, width = wq.shape[1], wq.shape[2]
    weight_spec = pl.BlockSpec(
        (None, None, width, width), lambda k, h, which, me, ids: (which[k], h, 0, 0)
    )
    block_spec = pl.BlockSpec(
        (None, *blocks[0].shape[1:]), lambda k, h, which, me, ids: (k, 0, 0, 0)
    )
    return pl.pallas_call(
        attention_send_kernel,
        out_shape=[jax.ShapeDtypeStruct((slots, heads, BLK, width), BF)] * size,
        grid_spec=pltpu.PrefetchScalarGridSpec(
            num_scalar_prefetch=3,
            grid=(slots, heads),
            in_specs=[block_spec] * size
            + [
                pl.BlockSpec(
                    (1, 1, width),
                    lambda k, h, which, me, ids: (which[k], 0, me[0] * heads + h),
                ),
                weight_spec,
                weight_spec,
                weight_spec,
            ],
            out_specs=[
                pl.BlockSpec((None, None, BLK, width), lambda k, h, which, me, ids: (k, h, 0, 0))
            ]
            * size,
            scratch_shapes=attention_scratch(size * BLK, width),
        ),
        cost_estimate=attention_cost(slots, heads, size, BLK, width),
        name="attention_send",
    )(which, me, ids, *blocks, gain, wq, wk, wv)


def mix_final_kernel(which, me, target, *refs):
    size = (len(refs) - 4) // 2
    att_refs, x_refs, w_ref = refs[:size], refs[size : 2 * size], refs[2 * size]
    out_ref, wide_ref, state_ref = refs[-3:]
    heads, rows, width = wide_ref.shape
    per = att_refs[0].shape[0]
    tile = x_refs[0].shape[1]
    tiles = rows // tile
    for k in range(size):
        group = me[0] ^ k
        for h in range(per):
            wide_ref[group * per + h] = att_refs[k][h].astype(F32)
            state = x_refs[k][h * tiles : (h + 1) * tiles]
            state_ref[group * per + h] = state.reshape(rows, width)
    step = 4

    def body(i, carry):
        totals = mix_totals(wide_ref, w_ref, i, step)
        for k in range(step):
            g = i * step + k
            lanes = pl.ds(pl.multiple_of(g * width, width), width)
            out_ref[:, lanes] = (state_ref[g].astype(F32) + totals[k]).astype(BF)
        return carry

    lax.fori_loop(0, heads // step, body, 0)


def mix_final(which, me, target, attended, states, weights):
    size = len(attended)
    slots, per, rows, width = attended[0].shape
    heads = size * per
    pairs = weights.shape[1]
    return pl.pallas_call(
        mix_final_kernel,
        out_shape=jax.ShapeDtypeStruct((slots, rows, heads * width), BF),
        grid_spec=pltpu.PrefetchScalarGridSpec(
            num_scalar_prefetch=3,
            grid=(slots,),
            in_specs=[
                pl.BlockSpec((None, *array.shape[1:]), lambda k, which, me, target: (k, 0, 0, 0))
                for array in [*attended, *states]
            ]
            + [pl.BlockSpec((1, pairs, width), lambda k, which, me, target: (which[k], 0, 0))],
            out_specs=pl.BlockSpec(
                (None, rows, heads * width), lambda k, which, me, target: (target[k], 0, 0)
            ),
            scratch_shapes=[
                pltpu.VMEM((heads, rows, width), F32),
                pltpu.VMEM((heads, rows, width), BF),
            ],
        ),
        cost_estimate=mix_cost(slots, rows, heads * width, pairs, width),
        name="mix_final",
    )(which, me, target, *attended, *states, weights)


def exchange(value):
    return lax.all_to_all(value, "fsdp", split_axis=0, concat_axis=0, tiled=True)


def send_on(blocks):
    segments, size = lax.axis_size("segment"), lax.axis_size("fsdp")
    arrived = []
    for k, block in enumerate(blocks):
        pairs = []
        for s in range(segments):
            for f in range(size):
                pairs.append((s * size + f, (s + 1) % segments * size + (f ^ k)))
        arrived.append(lax.ppermute(block, ("segment", "fsdp"), pairs))
    return arrived


def shifted(value):
    devices = lax.axis_size("segment")
    return lax.ppermute(value, "segment", [(i, (i + 1) % devices) for i in range(devices)])


def tie(value, *others):
    return lax.optimization_barrier((value, *others))[0]


def shards(stream, gain, w_query, w_key, w_value, w_mix, active, random_blocks):
    segments = lax.axis_size("segment")
    segment = lax.axis_index("segment")
    size = lax.axis_size("fsdp")
    slots = stream.shape[0]
    me = lax.axis_index("fsdp").astype(jnp.int32).reshape(1)
    wq, wk, wv = w_query[:, 0], w_key[:, 0], w_value[:, 0]
    ids = random_blocks[:, 0].reshape(-1)
    whole = stream[:, 0]

    def layers_of(place, turn):
        turned = jnp.where(place < turn, 1, 0)
        return ((jnp.arange(slots, dtype=jnp.int32) + turned) % slots).astype(jnp.int32)

    first = layers_of(segment, 0)
    second = layers_of(segment, 1)
    mixing = layers_of((segment + segments - 1) % segments, 1)
    target = layers_of(segment, 2)

    live = (active[:, 0] > 0)[:, None, None, None]
    masked = jnp.where(live, w_mix[:, 0], jnp.zeros_like(w_mix[:, 0]))
    masked = masked.reshape(1, slots, masked.shape[1], -1)
    bits = [1 << b for b in reversed(range(size.bit_length() - 1))]
    place = gathered_place(bits)

    own = partner(masked, bits[0])
    left = shifted(masked)
    normed = norm(first, whole, gain, size)
    own = partner(own, bits[1])
    rows = exchange(tie(normed, own, left))
    own = partner(tie(own, rows), bits[2])
    left = partner(tie(left, rows), bits[0])
    attended = attention(first, ids, rows, wq, wk, wv)
    back = exchange(tie(attended, own, left))
    own = mix_weights(place, own)
    left = partner(tie(left, back), bits[1])
    sent = mix_send(first, me, back, own, whole)
    sent = list(lax.optimization_barrier((*sent, left))[:-1])
    here = send_on(sent)
    onward = send_on(here)
    left = partner(tie(left, *here), bits[2])
    ready = lax.optimization_barrier((*here, *onward[:EARLY]))[: len(here)]
    attended = attention_send(second, me, ids, ready, gain, wq, wk, wv)
    last = send_on(lax.optimization_barrier((*attended, left))[:-1])
    left = mix_weights(place, left)
    done = mix_final(mixing, me, target, last, onward, left)
    return done[:, None]


def solution(mesh):
    in_specs = (
        P(None, "segment", "fsdp", None),
        P(None, "segment", None),
        P(None, "segment", "fsdp", None, None),
        P(None, "segment", "fsdp", None, None),
        P(None, "segment", "fsdp", None, None),
        P(None, "segment", "fsdp", None, None),
        P(None, "segment"),
        P(None, "segment", None, None),
    )
    out_specs = P(None, "segment", "fsdp", None)
    return jax.shard_map(shards, mesh=mesh, in_specs=in_specs, out_specs=out_specs, check_vma=False)
```

```python
import jax
import jax.numpy as jnp
from jax import lax
from jax.experimental import pallas as pl
from jax.experimental.pallas import tpu as pltpu
from jax.sharding import PartitionSpec as P

BLK = 64
EPS = 1e-05
BF = jnp.bfloat16
F32 = jnp.float32


def norm_kernel(which, x_ref, gain_ref, out_ref):
    groups, rows, width = out_ref.shape
    for start in range(0, rows, 16):
        wide = x_ref[start : start + 16, :].astype(F32)
        mean_sq = jnp.mean(wide * wide, axis=1, keepdims=True)
        normed = wide * lax.rsqrt(mean_sq + EPS) * gain_ref[0].astype(F32)
        normed = normed.astype(BF)
        for group in range(groups):
            out_ref[group, start : start + 16, :] = normed[:, group * width : (group + 1) * width]


def norm(which, x, gain, groups):
    slots, rows, features = x.shape
    width = features // groups
    return pl.pallas_call(
        norm_kernel,
        out_shape=jax.ShapeDtypeStruct((groups, slots, rows, width), BF),
        grid_spec=pltpu.PrefetchScalarGridSpec(
            num_scalar_prefetch=1,
            grid=(slots,),
            in_specs=[
                pl.BlockSpec((None, rows, features), lambda k, which: (k, 0, 0)),
                pl.BlockSpec((1, 1, features), lambda k, which: (which[k], 0, 0)),
            ],
            out_specs=pl.BlockSpec((groups, None, rows, width), lambda k, which: (0, k, 0, 0)),
        ),
        cost_estimate=pl.CostEstimate(
            flops=slots * rows * features * 6,
            bytes_accessed=slots * rows * features * 4,
            transcendentals=slots * rows,
        ),
        name="norm",
    )(which, x, gain)


def attend(wq, wk, wv, rows_ref, s_ref, p_ref, block, ids, base):
    keys = s_ref.shape[1]
    width = rows_ref.shape[1]
    count = keys // block
    picks = ids.shape[0] // (2 * count)
    rows = rows_ref[...]
    query = jnp.dot(rows, wq, preferred_element_type=F32)
    query = (query * width ** (-0.5)).astype(BF)
    key = jnp.dot(rows, wk, preferred_element_type=F32).astype(BF)
    value = jnp.dot(rows, wv, preferred_element_type=F32).astype(BF)
    s_ref[...] = lax.dot_general(query, key, (((1,), (1,)), ((), ())), preferred_element_type=F32)
    listed = lax.broadcasted_iota(jnp.int32, (8, keys), 1) // block
    totals = []
    for i in range(count):
        times = jnp.zeros((8, keys), F32)
        near = [(i - 1) % count, i, (i + 1) % count, 0]
        for b in near + [ids[base + i * picks + r] for r in range(picks)]:
            times = times + (listed == b).astype(F32)
        times = times[:1]
        at = slice(i * block, (i + 1) * block)
        scores = jnp.where(times > 0, s_ref[at, :], -jnp.inf)
        powers = jnp.exp(scores - jnp.max(scores, axis=1, keepdims=True)) * times
        totals.append(jnp.sum(powers, axis=1, keepdims=True))
        p_ref[at, :] = powers.astype(BF)
    mixed = jnp.dot(p_ref[...], value, preferred_element_type=F32)
    return (mixed / jnp.concatenate(totals, axis=0)).astype(BF)


def attention_kernel(which, ids, in_ref, wq_ref, wk_ref, wv_ref, out_ref, *scratch):
    rows_ref = scratch[0]
    count, block, width = in_ref.shape
    rows_ref[...] = in_ref[...].reshape(count * block, width)
    base = which[pl.program_id(0)] * (ids.shape[0] // 2)
    mixed = attend(wq_ref[...], wk_ref[...], wv_ref[...], *scratch, block, ids, base)
    out_ref[...] = mixed.reshape(count, block, width)


def attention_scratch(rows, width):
    return [pltpu.VMEM((rows, width), BF), pltpu.VMEM((rows, rows), F32), pltpu.VMEM((rows, rows), BF)]


def attention_cost(slots, heads, count, block, width):
    return pl.CostEstimate(
        flops=slots * heads * count * block * width * (6 * width + 4 * 6 * block),
        bytes_accessed=slots * heads * (count * block * width * 4 + width * width * 6),
        transcendentals=slots * heads * count * block * 6 * block,
    )


def attention(which, ids, rows, wq, wk, wv):
    count, slots, block, features = rows.shape
    heads, width = wq.shape[1], wq.shape[2]
    weight_spec = pl.BlockSpec(
        (None, None, width, width), lambda k, h, which, ids: (which[k], h, 0, 0)
    )
    row_spec = pl.BlockSpec((count, None, block, width), lambda k, h, which, ids: (0, k, 0, h))
    return pl.pallas_call(
        attention_kernel,
        out_shape=jax.ShapeDtypeStruct(rows.shape, BF),
        grid_spec=pltpu.PrefetchScalarGridSpec(
            num_scalar_prefetch=2,
            grid=(slots, heads),
            in_specs=[row_spec, weight_spec, weight_spec, weight_spec],
            out_specs=row_spec,
            scratch_shapes=attention_scratch(count * block, width),
        ),
        cost_estimate=attention_cost(slots, heads, count, block, width),
        name="attention",
    )(which, ids, rows, wq, wk, wv)


def mix_weights_kernel(place, gathered_ref, out_ref):
    groups = gathered_ref.shape[0]
    for v in range(out_ref.shape[0]):
        rows = jnp.concatenate([gathered_ref[place[j], v] for j in range(groups)], axis=0)
        out_ref[v] = rows.astype(F32).T


def partner(value, bit):
    size = lax.axis_size("fsdp")
    other = lax.ppermute(value, "fsdp", [(i, i ^ bit) for i in range(size)])
    return jnp.concatenate([value, other], axis=0)


def gathered_place(bits):
    order = [0]
    for bit in bits:
        order = order + [o ^ bit for o in order]
    back = [0] * len(order)
    for position, o in enumerate(order):
        back[o] = position
    me = lax.axis_index("fsdp")
    return jnp.array(back, jnp.int32)[jnp.arange(len(order), dtype=jnp.int32) ^ me]


def mix_weights(place, held):
    size, layers, mine, pairs = held.shape
    return pl.pallas_call(
        mix_weights_kernel,
        out_shape=jax.ShapeDtypeStruct((layers, pairs, mine * size), F32),
        grid_spec=pltpu.PrefetchScalarGridSpec(
            num_scalar_prefetch=1,
            grid=(1,),
            in_specs=[pl.BlockSpec(held.shape, lambda i, place: (0, 0, 0, 0))],
            out_specs=pl.BlockSpec((layers, pairs, mine * size), lambda i, place: (0, 0, 0)),
        ),
        name="mix_weights",
    )(place, held)


def mix_totals(wide_ref, w_ref, i, step):
    heads, rows, width = wide_ref.shape
    totals = [jnp.zeros((rows, width), F32) for _ in range(step)]
    for h in range(heads):
        attended = wide_ref[h]
        for k in range(step):
            row = w_ref[0, pl.ds(h * heads + i * step + k, 1), :]
            totals[k] = totals[k] + attended * row
    return [total.astype(BF).astype(F32) for total in totals]


def mix_send_kernel(which, me, att_ref, w_ref, x_ref, *refs):
    out_refs, (wide_ref, state_ref) = refs[:-2], refs[-2:]
    groups, rows, features = att_ref.shape
    width = w_ref.shape[2]
    per = features // width
    heads = groups * per
    tile = out_refs[0].shape[1]
    tiles = rows // tile
    for h in range(heads):
        lanes = pl.ds(h % per * width, width)
        wide_ref[h] = att_ref[h // per, :, lanes].astype(F32)
    step = 4

    def body(i, squares):
        totals = mix_totals(wide_ref, w_ref, i, step)
        for k in range(step):
            g = i * step + k
            lanes = pl.ds(pl.multiple_of(g * width, width), width)
            updated = (x_ref[:, lanes].astype(F32) + totals[k]).astype(BF)
            state_ref[g] = updated
            wide = updated.astype(F32)
            squares = squares + wide * wide
        return squares

    squares = lax.fori_loop(0, heads // step, body, jnp.zeros((rows, width), F32))
    mean_sq = jnp.sum(squares, axis=1, keepdims=True) / (heads * width)
    scale = lax.rsqrt(mean_sq + EPS)
    lane = lax.broadcasted_iota(jnp.int32, (tile, width), 1)
    packed = jnp.zeros((tile, width), F32)
    for t in range(tiles):
        rest = scale[t * tile : (t + 1) * tile]
        for term in range(3):
            top = rest.astype(BF).astype(F32)
            packed = jnp.where(lane == t * 4 + term, top, packed)
            rest = rest - top
    packed = packed.astype(BF)
    for r, out_ref in enumerate(out_refs):
        group = me[0] ^ r
        for h in range(per):
            out_ref[h * tiles : (h + 1) * tiles] = state_ref[group * per + h].reshape(
                tiles, tile, width
            )
        out_ref[per * tiles] = packed


def mix_cost(slots, rows, features, pairs, width):
    return pl.CostEstimate(
        flops=slots * rows * pairs * width * 2,
        bytes_accessed=slots * (rows * features * 6 + pairs * width * 4),
        transcendentals=0,
    )


def mix_send(which, me, attended, weights, x):
    slots, rows, features = x.shape
    groups = attended.shape[0]
    pairs, width = weights.shape[1:]
    tile = 16
    share = features // groups
    block = (rows // tile * (share // width) + 1, tile, width)
    heads = features // width
    return pl.pallas_call(
        mix_send_kernel,
        out_shape=[jax.ShapeDtypeStruct((slots, *block), BF)] * groups,
        grid_spec=pltpu.PrefetchScalarGridSpec(
            num_scalar_prefetch=2,
            grid=(slots,),
            in_specs=[
                pl.BlockSpec((groups, None, rows, share), lambda k, which, me: (0, k, 0, 0)),
                pl.BlockSpec((1, pairs, width), lambda k, which, me: (which[k], 0, 0)),
                pl.BlockSpec((None, rows, features), lambda k, which, me: (k, 0, 0)),
            ],
            out_specs=[pl.BlockSpec((None, *block), lambda k, which, me: (k, 0, 0, 0))] * groups,
            scratch_shapes=[
                pltpu.VMEM((heads, rows, width), F32),
                pltpu.VMEM((heads, rows, width), BF),
            ],
        ),
        cost_estimate=mix_cost(slots, rows, features, pairs, width),
        name="mix_send",
    )(which, me, attended, weights, x)


def attention_send_kernel(which, me, ids, *refs):
    size = (len(refs) - 7) // 2
    in_refs, rest = refs[:size], refs[size:]
    gain_ref, wq_ref, wk_ref, wv_ref = rest[:4]
    out_refs, scratch = rest[4:-3], rest[-3:]
    rows_ref = scratch[0]
    slot, head = pl.program_id(0), pl.program_id(1)
    block, width = out_refs[0].shape[1:]
    tile = in_refs[0].shape[1]
    tiles = block // tile
    gain = gain_ref[0].astype(F32)
    for k, ref in enumerate(in_refs):
        start = pl.multiple_of((me[0] ^ k) * block, block)
        rows = ref[pl.ds(head * tiles, tiles)].reshape(block, width)
        out_refs[k][1] = rows
        packed = ref[ref.shape[0] - 1].astype(F32)
        scale = jnp.concatenate(
            [
                packed[:, 4 * t : 4 * t + 1]
                + packed[:, 4 * t + 1 : 4 * t + 2]
                + packed[:, 4 * t + 2 : 4 * t + 3]
                for t in range(tiles)
            ],
            axis=0,
        )
        rows_ref[pl.ds(start, block), :] = (rows.astype(F32) * scale * gain).astype(BF)
    base = which[slot] * (ids.shape[0] // 2)
    mixed = attend(wq_ref[...], wk_ref[...], wv_ref[...], *scratch, block, ids, base)
    rows_ref[...] = mixed
    for k, out_ref in enumerate(out_refs):
        start = pl.multiple_of((me[0] ^ k) * block, block)
        out_ref[0] = rows_ref[pl.ds(start, block), :]


def attention_send(which, me, ids, blocks, gain, wq, wk, wv):
    size = len(blocks)
    slots = blocks[0].shape[0]
    heads, width = wq.shape[1], wq.shape[2]
    weight_spec = pl.BlockSpec(
        (None, None, width, width), lambda k, h, which, me, ids: (which[k], h, 0, 0)
    )
    block_spec = pl.BlockSpec(
        (None, *blocks[0].shape[1:]), lambda k, h, which, me, ids: (k, 0, 0, 0)
    )
    return pl.pallas_call(
        attention_send_kernel,
        out_shape=[jax.ShapeDtypeStruct((slots, 2, heads, BLK, width), BF)] * size,
        grid_spec=pltpu.PrefetchScalarGridSpec(
            num_scalar_prefetch=3,
            grid=(slots, heads),
            in_specs=[block_spec] * size
            + [
                pl.BlockSpec(
                    (1, 1, width),
                    lambda k, h, which, me, ids: (which[k], 0, me[0] * heads + h),
                ),
                weight_spec,
                weight_spec,
                weight_spec,
            ],
            out_specs=[
                pl.BlockSpec(
                    (None, 2, None, BLK, width), lambda k, h, which, me, ids: (k, 0, h, 0, 0)
                )
            ]
            * size,
            scratch_shapes=attention_scratch(size * BLK, width),
        ),
        cost_estimate=attention_cost(slots, heads, size, BLK, width),
        name="attention_send",
    )(which, me, ids, *blocks, gain, wq, wk, wv)


def mix_final_kernel(which, me, target, *refs):
    in_refs, (w_ref, out_ref, wide_ref, state_ref) = refs[:-4], refs[-4:]
    heads = wide_ref.shape[0]
    width = wide_ref.shape[2]
    per = in_refs[0].shape[1]
    for k, in_ref in enumerate(in_refs):
        group = me[0] ^ k
        for h in range(per):
            wide_ref[group * per + h] = in_ref[0, h].astype(F32)
            state_ref[group * per + h] = in_ref[1, h]
    step = 4

    def body(i, carry):
        totals = mix_totals(wide_ref, w_ref, i, step)
        for k in range(step):
            g = i * step + k
            lanes = pl.ds(pl.multiple_of(g * width, width), width)
            out_ref[:, lanes] = (state_ref[g].astype(F32) + totals[k]).astype(BF)
        return carry

    lax.fori_loop(0, heads // step, body, 0)


def mix_final(which, me, target, blocks, weights):
    size = len(blocks)
    slots, _, per, rows, width = blocks[0].shape
    heads = size * per
    pairs = weights.shape[1]
    return pl.pallas_call(
        mix_final_kernel,
        out_shape=jax.ShapeDtypeStruct((slots, rows, heads * width), BF),
        grid_spec=pltpu.PrefetchScalarGridSpec(
            num_scalar_prefetch=3,
            grid=(slots,),
            in_specs=[
                pl.BlockSpec(
                    (None, *blocks[0].shape[1:]), lambda k, which, me, target: (k, 0, 0, 0, 0)
                )
            ]
            * size
            + [pl.BlockSpec((1, pairs, width), lambda k, which, me, target: (which[k], 0, 0))],
            out_specs=pl.BlockSpec(
                (None, rows, heads * width), lambda k, which, me, target: (target[k], 0, 0)
            ),
            scratch_shapes=[
                pltpu.VMEM((heads, rows, width), F32),
                pltpu.VMEM((heads, rows, width), BF),
            ],
        ),
        cost_estimate=mix_cost(slots, rows, heads * width, pairs, width),
        name="mix_final",
    )(which, me, target, *blocks, weights)


def exchange(value):
    return lax.all_to_all(value, "fsdp", split_axis=0, concat_axis=0, tiled=True)


def send_on(blocks):
    segments, size = lax.axis_size("segment"), lax.axis_size("fsdp")
    arrived = []
    for k, block in enumerate(blocks):
        pairs = []
        for s in range(segments):
            for f in range(size):
                pairs.append((s * size + f, (s + 1) % segments * size + (f ^ k)))
        arrived.append(lax.ppermute(block, ("segment", "fsdp"), pairs))
    return arrived


def shifted(value):
    devices = lax.axis_size("segment")
    return lax.ppermute(value, "segment", [(i, (i + 1) % devices) for i in range(devices)])


def tie(value, *others):
    return lax.optimization_barrier((value, *others))[0]


def shards(stream, gain, w_query, w_key, w_value, w_mix, active, random_blocks):
    segments = lax.axis_size("segment")
    segment = lax.axis_index("segment")
    size = lax.axis_size("fsdp")
    slots = stream.shape[0]
    me = lax.axis_index("fsdp").astype(jnp.int32).reshape(1)
    wq, wk, wv = w_query[:, 0], w_key[:, 0], w_value[:, 0]
    ids = random_blocks[:, 0].reshape(-1)
    whole = stream[:, 0]

    def layers_of(place, turn):
        turned = jnp.where(place < turn, 1, 0)
        return ((jnp.arange(slots, dtype=jnp.int32) + turned) % slots).astype(jnp.int32)

    first = layers_of(segment, 0)
    second = layers_of(segment, 1)
    mixing = layers_of((segment + segments - 1) % segments, 1)
    target = layers_of(segment, 2)

    live = (active[:, 0] > 0)[:, None, None, None]
    masked = jnp.where(live, w_mix[:, 0], jnp.zeros_like(w_mix[:, 0]))
    masked = masked.reshape(1, slots, masked.shape[1], -1)
    bits = [1 << b for b in reversed(range(size.bit_length() - 1))]
    place = gathered_place(bits)

    own = partner(masked, bits[0])
    normed = norm(first, whole, gain, size)
    rows = exchange(tie(normed, own))
    own = partner(own, bits[1])
    left = shifted(tie(masked, normed))
    rows = tie(rows, own, left)
    own = partner(tie(own, rows), bits[2])
    left = partner(tie(left, rows), bits[0])
    attended = attention(first, ids, rows, wq, wk, wv)
    back = exchange(tie(attended, own, left))
    own = mix_weights(place, own)
    left = partner(left, bits[1])
    back = tie(back, left, own)
    left = partner(tie(left, back), bits[2])
    sent = mix_send(first, me, back, own, whole)
    sent = list(lax.optimization_barrier((*sent, left))[:-1])
    here = send_on(sent)
    attended = attention_send(second, me, ids, here, gain, wq, wk, wv)
    left = mix_weights(place, left)
    last = send_on(attended)
    done = mix_final(mixing, me, target, last, left)
    return done[:, None]


def solution(mesh):
    in_specs = (
        P(None, "segment", "fsdp", None),
        P(None, "segment", None),
        P(None, "segment", "fsdp", None, None),
        P(None, "segment", "fsdp", None, None),
        P(None, "segment", "fsdp", None, None),
        P(None, "segment", "fsdp", None, None),
        P(None, "segment"),
        P(None, "segment", None, None),
    )
    out_specs = P(None, "segment", "fsdp", None)
    return jax.shard_map(shards, mesh=mesh, in_specs=in_specs, out_specs=out_specs, check_vma=False)
```

```python
import jax
import jax.numpy as jnp
from jax import lax
from jax.experimental import pallas as pl
from jax.experimental.pallas import tpu as pltpu
from jax.sharding import PartitionSpec as P

BLK = 64
EPS = 1e-05
BF = jnp.bfloat16
F32 = jnp.float32


def norm_kernel(which, x_ref, gain_ref, out_ref):
    groups, rows, width = out_ref.shape
    for start in range(0, rows, 16):
        wide = x_ref[start : start + 16, :].astype(F32)
        mean_sq = jnp.mean(wide * wide, axis=1, keepdims=True)
        normed = wide * lax.rsqrt(mean_sq + EPS) * gain_ref[0].astype(F32)
        normed = normed.astype(BF)
        for group in range(groups):
            out_ref[group, start : start + 16, :] = normed[:, group * width : (group + 1) * width]


def norm(which, x, gain, groups):
    slots, rows, features = x.shape
    width = features // groups
    return pl.pallas_call(
        norm_kernel,
        out_shape=jax.ShapeDtypeStruct((groups, slots, rows, width), BF),
        grid_spec=pltpu.PrefetchScalarGridSpec(
            num_scalar_prefetch=1,
            grid=(slots,),
            in_specs=[
                pl.BlockSpec((None, rows, features), lambda k, which: (k, 0, 0)),
                pl.BlockSpec((1, 1, features), lambda k, which: (which[k], 0, 0)),
            ],
            out_specs=pl.BlockSpec((groups, None, rows, width), lambda k, which: (0, k, 0, 0)),
        ),
        cost_estimate=pl.CostEstimate(
            flops=slots * rows * features * 6,
            bytes_accessed=slots * rows * features * 4,
            transcendentals=slots * rows,
        ),
        name="norm",
    )(which, x, gain)


def attend(wq, wk, wv, rows_ref, s_ref, p_ref, block, ids, base):
    keys = s_ref.shape[1]
    width = rows_ref.shape[1]
    count = keys // block
    picks = ids.shape[0] // (2 * count)
    rows = rows_ref[...]
    raw = jnp.dot(rows, jnp.concatenate([wq, wk, wv], axis=1), preferred_element_type=F32)
    query = (raw[:, :width] * width ** (-0.5)).astype(BF)
    key = raw[:, width : 2 * width].astype(BF)
    value = raw[:, 2 * width :].astype(BF)
    s_ref[...] = lax.dot_general(query, key, (((1,), (1,)), ((), ())), preferred_element_type=F32)
    listed = lax.broadcasted_iota(jnp.int32, (8, keys), 1) // block
    for i in range(count):
        times = jnp.zeros((8, keys), F32)
        near = [(i - 1) % count, i, (i + 1) % count, 0]
        for b in near + [ids[base + i * picks + r] for r in range(picks)]:
            times = times + (listed == b).astype(F32)
        times = times[:1]
        at = slice(i * block, (i + 1) * block)
        scores = jnp.where(times > 0, s_ref[at, :], -jnp.inf)
        powers = jnp.exp(scores - jnp.max(scores, axis=1, keepdims=True)) * times
        p_ref[at, :] = powers.astype(BF)
    value = jnp.concatenate([value, jnp.ones_like(value)], axis=1)
    mixed = jnp.dot(p_ref[...], value, preferred_element_type=F32)
    return (mixed[:, :width] / mixed[:, width:]).astype(BF)


def attention_kernel(which, ids, in_ref, wq_ref, wk_ref, wv_ref, out_ref, *scratch):
    rows_ref = scratch[0]
    count, block, width = in_ref.shape
    rows_ref[...] = in_ref[...].reshape(count * block, width)
    base = which[pl.program_id(0)] * (ids.shape[0] // 2)
    mixed = attend(wq_ref[...], wk_ref[...], wv_ref[...], *scratch, block, ids, base)
    out_ref[...] = mixed.reshape(count, block, width)


def attention_scratch(rows, width):
    return [pltpu.VMEM((rows, width), BF), pltpu.VMEM((rows, rows), F32), pltpu.VMEM((rows, rows), BF)]


def attention_cost(slots, heads, count, block, width):
    return pl.CostEstimate(
        flops=slots * heads * count * block * width * (6 * width + 4 * 6 * block),
        bytes_accessed=slots * heads * (count * block * width * 4 + width * width * 6),
        transcendentals=slots * heads * count * block * 6 * block,
    )


def attention(which, ids, rows, wq, wk, wv):
    count, slots, block, features = rows.shape
    heads, width = wq.shape[1], wq.shape[2]
    weight_spec = pl.BlockSpec(
        (None, None, width, width), lambda k, h, which, ids: (which[k], h, 0, 0)
    )
    row_spec = pl.BlockSpec((count, None, block, width), lambda k, h, which, ids: (0, k, 0, h))
    return pl.pallas_call(
        attention_kernel,
        out_shape=jax.ShapeDtypeStruct(rows.shape, BF),
        grid_spec=pltpu.PrefetchScalarGridSpec(
            num_scalar_prefetch=2,
            grid=(slots, heads),
            in_specs=[row_spec, weight_spec, weight_spec, weight_spec],
            out_specs=row_spec,
            scratch_shapes=attention_scratch(count * block, width),
        ),
        cost_estimate=attention_cost(slots, heads, count, block, width),
        name="attention",
    )(which, ids, rows, wq, wk, wv)


def mix_weights_kernel(place, gathered_ref, out_ref):
    groups = gathered_ref.shape[0]
    for v in range(out_ref.shape[0]):
        rows = jnp.concatenate([gathered_ref[place[j], v] for j in range(groups)], axis=0)
        out_ref[v] = rows.astype(F32).T


def partner(value, bit):
    size = lax.axis_size("fsdp")
    other = lax.ppermute(value, "fsdp", [(i, i ^ bit) for i in range(size)])
    return jnp.concatenate([value, other], axis=0)


def gathered_place(bits):
    order = [0]
    for bit in bits:
        order = order + [o ^ bit for o in order]
    back = [0] * len(order)
    for position, o in enumerate(order):
        back[o] = position
    me = lax.axis_index("fsdp")
    return jnp.array(back, jnp.int32)[jnp.arange(len(order), dtype=jnp.int32) ^ me]


def mix_weights(place, held):
    size, layers, mine, pairs = held.shape
    return pl.pallas_call(
        mix_weights_kernel,
        out_shape=jax.ShapeDtypeStruct((layers, pairs, mine * size), F32),
        grid_spec=pltpu.PrefetchScalarGridSpec(
            num_scalar_prefetch=1,
            grid=(1,),
            in_specs=[pl.BlockSpec(held.shape, lambda i, place: (0, 0, 0, 0))],
            out_specs=pl.BlockSpec((layers, pairs, mine * size), lambda i, place: (0, 0, 0)),
        ),
        name="mix_weights",
    )(place, held)


def mix_totals(wide_ref, w_ref, i, step):
    heads, rows, width = wide_ref.shape
    totals = [jnp.zeros((rows, width), F32) for _ in range(step)]
    for h in range(heads):
        attended = wide_ref[h]
        for k in range(step):
            row = w_ref[0, pl.ds(h * heads + i * step + k, 1), :]
            totals[k] = totals[k] + attended * row
    return [total.astype(BF).astype(F32) for total in totals]


def mix_send_kernel(which, me, att_ref, w_ref, x_ref, *refs):
    out_refs, (wide_ref, state_ref) = refs[:-2], refs[-2:]
    groups, rows, features = att_ref.shape
    width = w_ref.shape[2]
    per = features // width
    heads = groups * per
    tile = out_refs[0].shape[1]
    tiles = rows // tile
    for h in range(heads):
        lanes = pl.ds(h % per * width, width)
        wide_ref[h] = att_ref[h // per, :, lanes].astype(F32)
    step = 4

    def body(i, squares):
        totals = mix_totals(wide_ref, w_ref, i, step)
        for k in range(step):
            g = i * step + k
            lanes = pl.ds(pl.multiple_of(g * width, width), width)
            updated = (x_ref[:, lanes].astype(F32) + totals[k]).astype(BF)
            state_ref[g] = updated
            wide = updated.astype(F32)
            squares = squares + wide * wide
        return squares

    squares = lax.fori_loop(0, heads // step, body, jnp.zeros((rows, width), F32))
    mean_sq = jnp.sum(squares, axis=1, keepdims=True) / (heads * width)
    scale = lax.rsqrt(mean_sq + EPS)
    lane = lax.broadcasted_iota(jnp.int32, (tile, width), 1)
    packed = jnp.zeros((tile, width), F32)
    for t in range(tiles):
        rest = scale[t * tile : (t + 1) * tile]
        for term in range(3):
            top = rest.astype(BF).astype(F32)
            packed = jnp.where(lane == t * 4 + term, top, packed)
            rest = rest - top
    packed = packed.astype(BF)
    for r, out_ref in enumerate(out_refs):
        group = me[0] ^ r
        for h in range(per):
            out_ref[h * tiles : (h + 1) * tiles] = state_ref[group * per + h].reshape(
                tiles, tile, width
            )
        out_ref[per * tiles] = packed


def mix_cost(slots, rows, features, pairs, width):
    return pl.CostEstimate(
        flops=slots * rows * pairs * width * 2,
        bytes_accessed=slots * (rows * features * 6 + pairs * width * 4),
        transcendentals=0,
    )


def mix_send(which, me, attended, weights, x):
    slots, rows, features = x.shape
    groups = attended.shape[0]
    pairs, width = weights.shape[1:]
    tile = 16
    share = features // groups
    block = (rows // tile * (share // width) + 1, tile, width)
    heads = features // width
    return pl.pallas_call(
        mix_send_kernel,
        out_shape=[jax.ShapeDtypeStruct((slots, *block), BF)] * groups,
        grid_spec=pltpu.PrefetchScalarGridSpec(
            num_scalar_prefetch=2,
            grid=(slots,),
            in_specs=[
                pl.BlockSpec((groups, None, rows, share), lambda k, which, me: (0, k, 0, 0)),
                pl.BlockSpec((1, pairs, width), lambda k, which, me: (which[k], 0, 0)),
                pl.BlockSpec((None, rows, features), lambda k, which, me: (k, 0, 0)),
            ],
            out_specs=[pl.BlockSpec((None, *block), lambda k, which, me: (k, 0, 0, 0))] * groups,
            scratch_shapes=[
                pltpu.VMEM((heads, rows, width), F32),
                pltpu.VMEM((heads, rows, width), BF),
            ],
        ),
        cost_estimate=mix_cost(slots, rows, features, pairs, width),
        name="mix_send",
    )(which, me, attended, weights, x)


def attention_send_kernel(which, me, ids, *refs):
    size = (len(refs) - 7) // 2
    in_refs, rest = refs[:size], refs[size:]
    gain_ref, wq_ref, wk_ref, wv_ref = rest[:4]
    out_refs, scratch = rest[4:-3], rest[-3:]
    rows_ref = scratch[0]
    slot, head = pl.program_id(0), pl.program_id(1)
    block, width = out_refs[0].shape[1:]
    tile = in_refs[0].shape[1]
    tiles = block // tile
    gain = gain_ref[0].astype(F32)
    for k, ref in enumerate(in_refs):
        start = pl.multiple_of((me[0] ^ k) * block, block)
        rows = ref[pl.ds(head * tiles, tiles)].reshape(block, width)
        out_refs[k][1] = rows
        packed = ref[ref.shape[0] - 1].astype(F32)
        scale = jnp.concatenate(
            [
                packed[:, 4 * t : 4 * t + 1]
                + packed[:, 4 * t + 1 : 4 * t + 2]
                + packed[:, 4 * t + 2 : 4 * t + 3]
                for t in range(tiles)
            ],
            axis=0,
        )
        rows_ref[pl.ds(start, block), :] = (rows.astype(F32) * scale * gain).astype(BF)
    base = which[slot] * (ids.shape[0] // 2)
    mixed = attend(wq_ref[...], wk_ref[...], wv_ref[...], *scratch, block, ids, base)
    rows_ref[...] = mixed
    for k, out_ref in enumerate(out_refs):
        start = pl.multiple_of((me[0] ^ k) * block, block)
        out_ref[0] = rows_ref[pl.ds(start, block), :]


def attention_send(which, me, ids, blocks, gain, wq, wk, wv):
    size = len(blocks)
    slots = blocks[0].shape[0]
    heads, width = wq.shape[1], wq.shape[2]
    weight_spec = pl.BlockSpec(
        (None, None, width, width), lambda k, h, which, me, ids: (which[k], h, 0, 0)
    )
    block_spec = pl.BlockSpec(
        (None, *blocks[0].shape[1:]), lambda k, h, which, me, ids: (k, 0, 0, 0)
    )
    return pl.pallas_call(
        attention_send_kernel,
        out_shape=[jax.ShapeDtypeStruct((slots, 2, heads, BLK, width), BF)] * size,
        grid_spec=pltpu.PrefetchScalarGridSpec(
            num_scalar_prefetch=3,
            grid=(slots, heads),
            in_specs=[block_spec] * size
            + [
                pl.BlockSpec(
                    (1, 1, width),
                    lambda k, h, which, me, ids: (which[k], 0, me[0] * heads + h),
                ),
                weight_spec,
                weight_spec,
                weight_spec,
            ],
            out_specs=[
                pl.BlockSpec(
                    (None, 2, None, BLK, width), lambda k, h, which, me, ids: (k, 0, h, 0, 0)
                )
            ]
            * size,
            scratch_shapes=attention_scratch(size * BLK, width),
        ),
        cost_estimate=attention_cost(slots, heads, size, BLK, width),
        name="attention_send",
    )(which, me, ids, *blocks, gain, wq, wk, wv)


def mix_final_kernel(which, me, target, *refs):
    in_refs, (w_ref, out_ref, wide_ref, state_ref) = refs[:-4], refs[-4:]
    heads = wide_ref.shape[0]
    width = wide_ref.shape[2]
    per = in_refs[0].shape[1]
    for k, in_ref in enumerate(in_refs):
        group = me[0] ^ k
        for h in range(per):
            wide_ref[group * per + h] = in_ref[0, h].astype(F32)
            state_ref[group * per + h] = in_ref[1, h]
    step = 4

    def body(i, carry):
        totals = mix_totals(wide_ref, w_ref, i, step)
        for k in range(step):
            g = i * step + k
            lanes = pl.ds(pl.multiple_of(g * width, width), width)
            out_ref[:, lanes] = (state_ref[g].astype(F32) + totals[k]).astype(BF)
        return carry

    lax.fori_loop(0, heads // step, body, 0)


def mix_final(which, me, target, blocks, weights):
    size = len(blocks)
    slots, _, per, rows, width = blocks[0].shape
    heads = size * per
    pairs = weights.shape[1]
    return pl.pallas_call(
        mix_final_kernel,
        out_shape=jax.ShapeDtypeStruct((slots, rows, heads * width), BF),
        grid_spec=pltpu.PrefetchScalarGridSpec(
            num_scalar_prefetch=3,
            grid=(slots,),
            in_specs=[
                pl.BlockSpec(
                    (None, *blocks[0].shape[1:]), lambda k, which, me, target: (k, 0, 0, 0, 0)
                )
            ]
            * size
            + [pl.BlockSpec((1, pairs, width), lambda k, which, me, target: (which[k], 0, 0))],
            out_specs=pl.BlockSpec(
                (None, rows, heads * width), lambda k, which, me, target: (target[k], 0, 0)
            ),
            scratch_shapes=[
                pltpu.VMEM((heads, rows, width), F32),
                pltpu.VMEM((heads, rows, width), BF),
            ],
        ),
        cost_estimate=mix_cost(slots, rows, heads * width, pairs, width),
        name="mix_final",
    )(which, me, target, *blocks, weights)


def exchange(value):
    return lax.all_to_all(value, "fsdp", split_axis=0, concat_axis=0, tiled=True)


def send_on(blocks):
    segments, size = lax.axis_size("segment"), lax.axis_size("fsdp")
    arrived = []
    for k, block in enumerate(blocks):
        pairs = []
        for s in range(segments):
            for f in range(size):
                pairs.append((s * size + f, (s + 1) % segments * size + (f ^ k)))
        arrived.append(lax.ppermute(block, ("segment", "fsdp"), pairs))
    return arrived


def shifted(value):
    devices = lax.axis_size("segment")
    return lax.ppermute(value, "segment", [(i, (i + 1) % devices) for i in range(devices)])


def tie(value, *others):
    return lax.optimization_barrier((value, *others))[0]


def shards(stream, gain, w_query, w_key, w_value, w_mix, active, random_blocks):
    segments = lax.axis_size("segment")
    segment = lax.axis_index("segment")
    size = lax.axis_size("fsdp")
    slots = stream.shape[0]
    me = lax.axis_index("fsdp").astype(jnp.int32).reshape(1)
    wq, wk, wv = w_query[:, 0], w_key[:, 0], w_value[:, 0]
    ids = random_blocks[:, 0].reshape(-1)
    whole = stream[:, 0]

    def layers_of(place, turn):
        turned = jnp.where(place < turn, 1, 0)
        return ((jnp.arange(slots, dtype=jnp.int32) + turned) % slots).astype(jnp.int32)

    first = layers_of(segment, 0)
    second = layers_of(segment, 1)
    mixing = layers_of((segment + segments - 1) % segments, 1)
    target = layers_of(segment, 2)

    live = (active[:, 0] > 0)[:, None, None, None]
    masked = jnp.where(live, w_mix[:, 0], jnp.zeros_like(w_mix[:, 0]))
    masked = masked.reshape(1, slots, masked.shape[1], -1)
    bits = [1 << b for b in reversed(range(size.bit_length() - 1))]
    place = gathered_place(bits)

    own = partner(masked, bits[0])
    normed = norm(first, whole, gain, size)
    rows = exchange(tie(normed, own))
    own = partner(own, bits[1])
    left = shifted(tie(masked, normed))
    rows = tie(rows, own, left)
    own = partner(tie(own, rows), bits[2])
    left = partner(tie(left, rows), bits[0])
    attended = attention(first, ids, rows, wq, wk, wv)
    back = exchange(tie(attended, own, left))
    own = mix_weights(place, own)
    left = partner(left, bits[1])
    back = tie(back, left, own)
    here = send_on(mix_send(first, me, back, own, whole))
    left = partner(tie(left, *here), bits[2])
    attended = attention_send(second, me, ids, here, gain, wq, wk, wv)
    left = mix_weights(place, left)
    last = send_on(attended)
    done = mix_final(mixing, me, target, last, left)
    return done[:, None]


def solution(mesh):
    in_specs = (
        P(None, "segment", "fsdp", None),
        P(None, "segment", None),
        P(None, "segment", "fsdp", None, None),
        P(None, "segment", "fsdp", None, None),
        P(None, "segment", "fsdp", None, None),
        P(None, "segment", "fsdp", None, None),
        P(None, "segment"),
        P(None, "segment", None, None),
    )
    out_specs = P(None, "segment", "fsdp", None)
    return jax.shard_map(shards, mesh=mesh, in_specs=in_specs, out_specs=out_specs, check_vma=False)
```

```python
import jax
import jax.numpy as jnp
from jax import lax
from jax.experimental import pallas as pl
from jax.experimental.pallas import tpu as pltpu
from jax.sharding import PartitionSpec as P

BLK = 64
EPS = 1e-05
BF = jnp.bfloat16
F32 = jnp.float32


def norm_kernel(which, x_ref, gain_ref, out_ref):
    groups, rows, width = out_ref.shape
    for start in range(0, rows, 16):
        wide = x_ref[start : start + 16, :].astype(F32)
        mean_sq = jnp.mean(wide * wide, axis=1, keepdims=True)
        normed = wide * lax.rsqrt(mean_sq + EPS) * gain_ref[0].astype(F32)
        normed = normed.astype(BF)
        for group in range(groups):
            out_ref[group, start : start + 16, :] = normed[:, group * width : (group + 1) * width]


def norm(which, x, gain, groups):
    slots, rows, features = x.shape
    width = features // groups
    return pl.pallas_call(
        norm_kernel,
        out_shape=jax.ShapeDtypeStruct((groups, slots, rows, width), BF),
        grid_spec=pltpu.PrefetchScalarGridSpec(
            num_scalar_prefetch=1,
            grid=(slots,),
            in_specs=[
                pl.BlockSpec((None, rows, features), lambda k, which: (k, 0, 0)),
                pl.BlockSpec((1, 1, features), lambda k, which: (which[k], 0, 0)),
            ],
            out_specs=pl.BlockSpec((groups, None, rows, width), lambda k, which: (0, k, 0, 0)),
        ),
        cost_estimate=pl.CostEstimate(
            flops=slots * rows * features * 6,
            bytes_accessed=slots * rows * features * 4,
            transcendentals=slots * rows,
        ),
        name="norm",
    )(which, x, gain)


def attend(wq, wk, wv, rows_ref, s_ref, p_ref, t_ref, block, ids, base):
    keys = s_ref.shape[1]
    width = rows_ref.shape[1]
    count = keys // block
    picks = ids.shape[0] // (2 * count)
    rows = rows_ref[...]
    raw = jnp.dot(rows, jnp.concatenate([wq, wk, wv], axis=1), preferred_element_type=F32)
    query = (raw[:, :width] * width ** (-0.5)).astype(BF)
    key = raw[:, width : 2 * width].astype(BF)
    value = raw[:, 2 * width :].astype(BF)
    s_ref[...] = lax.dot_general(query, key, (((1,), (1,)), ((), ())), preferred_element_type=F32)

    @pl.when(pl.program_id(1) == 0)
    def _():
        listed = lax.broadcasted_iota(jnp.int32, (8, keys), 1) // block
        for i in range(count):
            times = jnp.zeros((8, keys), F32)
            near = [(i - 1) % count, i, (i + 1) % count, 0]
            for b in near + [ids[base + i * picks + r] for r in range(picks)]:
                times = times + (listed == b).astype(F32)
            t_ref[i] = times

    for i in range(count):
        times = t_ref[i, :1]
        at = slice(i * block, (i + 1) * block)
        scores = jnp.where(times > 0, s_ref[at, :], -jnp.inf)
        powers = jnp.exp(scores - jnp.max(scores, axis=1, keepdims=True)) * times
        p_ref[at, :] = powers.astype(BF)
    value = jnp.concatenate([value, jnp.ones_like(value)], axis=1)
    mixed = jnp.dot(p_ref[...], value, preferred_element_type=F32)
    return (mixed[:, :width] / mixed[:, width:]).astype(BF)


def attention_kernel(which, ids, in_ref, wq_ref, wk_ref, wv_ref, out_ref, *scratch):
    rows_ref = scratch[0]
    count, block, width = in_ref.shape
    rows_ref[...] = in_ref[...].reshape(count * block, width)
    base = which[pl.program_id(0)] * (ids.shape[0] // 2)
    mixed = attend(wq_ref[...], wk_ref[...], wv_ref[...], *scratch, block, ids, base)
    out_ref[...] = mixed.reshape(count, block, width)


def attention_scratch(rows, width):
    return [
        pltpu.VMEM((rows, width), BF),
        pltpu.VMEM((rows, rows), F32),
        pltpu.VMEM((rows, rows), BF),
        pltpu.VMEM((rows // BLK, 8, rows), F32),
    ]


def attention_cost(slots, heads, count, block, width):
    return pl.CostEstimate(
        flops=slots * heads * count * block * width * (6 * width + 4 * 6 * block),
        bytes_accessed=slots * heads * (count * block * width * 4 + width * width * 6),
        transcendentals=slots * heads * count * block * 6 * block,
    )


def attention(which, ids, rows, wq, wk, wv):
    count, slots, block, features = rows.shape
    heads, width = wq.shape[1], wq.shape[2]
    weight_spec = pl.BlockSpec(
        (None, None, width, width), lambda k, h, which, ids: (which[k], h, 0, 0)
    )
    row_spec = pl.BlockSpec((count, None, block, width), lambda k, h, which, ids: (0, k, 0, h))
    return pl.pallas_call(
        attention_kernel,
        out_shape=jax.ShapeDtypeStruct(rows.shape, BF),
        grid_spec=pltpu.PrefetchScalarGridSpec(
            num_scalar_prefetch=2,
            grid=(slots, heads),
            in_specs=[row_spec, weight_spec, weight_spec, weight_spec],
            out_specs=row_spec,
            scratch_shapes=attention_scratch(count * block, width),
        ),
        cost_estimate=attention_cost(slots, heads, count, block, width),
        name="attention",
    )(which, ids, rows, wq, wk, wv)


def mix_weights_kernel(place, gathered_ref, out_ref):
    groups = gathered_ref.shape[0]
    for v in range(out_ref.shape[0]):
        rows = jnp.concatenate([gathered_ref[place[j], v] for j in range(groups)], axis=0)
        out_ref[v] = rows.astype(F32).T


def partner(value, bit):
    size = lax.axis_size("fsdp")
    other = lax.ppermute(value, "fsdp", [(i, i ^ bit) for i in range(size)])
    return jnp.concatenate([value, other], axis=0)


def gathered_place(bits):
    order = [0]
    for bit in bits:
        order = order + [o ^ bit for o in order]
    back = [0] * len(order)
    for position, o in enumerate(order):
        back[o] = position
    me = lax.axis_index("fsdp")
    return jnp.array(back, jnp.int32)[jnp.arange(len(order), dtype=jnp.int32) ^ me]


def mix_weights(place, held):
    size, layers, mine, pairs = held.shape
    return pl.pallas_call(
        mix_weights_kernel,
        out_shape=jax.ShapeDtypeStruct((layers, pairs, mine * size), F32),
        grid_spec=pltpu.PrefetchScalarGridSpec(
            num_scalar_prefetch=1,
            grid=(1,),
            in_specs=[pl.BlockSpec(held.shape, lambda i, place: (0, 0, 0, 0))],
            out_specs=pl.BlockSpec((layers, pairs, mine * size), lambda i, place: (0, 0, 0)),
        ),
        name="mix_weights",
    )(place, held)


def mix_totals(wide_ref, w_ref, i, step):
    heads, rows, width = wide_ref.shape
    totals = [jnp.zeros((rows, width), F32) for _ in range(step)]
    for h in range(heads):
        attended = wide_ref[h]
        for k in range(step):
            row = w_ref[0, pl.ds(h * heads + i * step + k, 1), :]
            totals[k] = totals[k] + attended * row
    return [total.astype(BF).astype(F32) for total in totals]


def mix_send_kernel(which, me, att_ref, w_ref, x_ref, *refs):
    out_refs, (wide_ref, state_ref) = refs[:-2], refs[-2:]
    groups, rows, features = att_ref.shape
    width = w_ref.shape[2]
    per = features // width
    heads = groups * per
    tile = out_refs[0].shape[1]
    tiles = rows // tile
    for h in range(heads):
        lanes = pl.ds(h % per * width, width)
        wide_ref[h] = att_ref[h // per, :, lanes].astype(F32)
    step = 4

    def body(i, squares):
        totals = mix_totals(wide_ref, w_ref, i, step)
        for k in range(step):
            g = i * step + k
            lanes = pl.ds(pl.multiple_of(g * width, width), width)
            updated = (x_ref[:, lanes].astype(F32) + totals[k]).astype(BF)
            state_ref[g] = updated
            wide = updated.astype(F32)
            squares = squares + wide * wide
        return squares

    squares = lax.fori_loop(0, heads // step, body, jnp.zeros((rows, width), F32))
    mean_sq = jnp.sum(squares, axis=1, keepdims=True) / (heads * width)
    scale = lax.rsqrt(mean_sq + EPS)
    lane = lax.broadcasted_iota(jnp.int32, (tile, width), 1)
    packed = jnp.zeros((tile, width), F32)
    for t in range(tiles):
        rest = scale[t * tile : (t + 1) * tile]
        for term in range(3):
            top = rest.astype(BF).astype(F32)
            packed = jnp.where(lane == t * 4 + term, top, packed)
            rest = rest - top
    packed = packed.astype(BF)
    for r, out_ref in enumerate(out_refs):
        group = me[0] ^ r
        for h in range(per):
            out_ref[h * tiles : (h + 1) * tiles] = state_ref[group * per + h].reshape(
                tiles, tile, width
            )
        out_ref[per * tiles] = packed


def mix_cost(slots, rows, features, pairs, width):
    return pl.CostEstimate(
        flops=slots * rows * pairs * width * 2,
        bytes_accessed=slots * (rows * features * 6 + pairs * width * 4),
        transcendentals=0,
    )


def mix_send(which, me, attended, weights, x):
    slots, rows, features = x.shape
    groups = attended.shape[0]
    pairs, width = weights.shape[1:]
    tile = 16
    share = features // groups
    block = (rows // tile * (share // width) + 1, tile, width)
    heads = features // width
    return pl.pallas_call(
        mix_send_kernel,
        out_shape=[jax.ShapeDtypeStruct((slots, *block), BF)] * groups,
        grid_spec=pltpu.PrefetchScalarGridSpec(
            num_scalar_prefetch=2,
            grid=(slots,),
            in_specs=[
                pl.BlockSpec((groups, None, rows, share), lambda k, which, me: (0, k, 0, 0)),
                pl.BlockSpec((1, pairs, width), lambda k, which, me: (which[k], 0, 0)),
                pl.BlockSpec((None, rows, features), lambda k, which, me: (k, 0, 0)),
            ],
            out_specs=[pl.BlockSpec((None, *block), lambda k, which, me: (k, 0, 0, 0))] * groups,
            scratch_shapes=[
                pltpu.VMEM((heads, rows, width), F32),
                pltpu.VMEM((heads, rows, width), BF),
            ],
        ),
        cost_estimate=mix_cost(slots, rows, features, pairs, width),
        name="mix_send",
    )(which, me, attended, weights, x)


def attention_send_kernel(which, me, ids, *refs):
    size = (len(refs) - 8) // 2
    in_refs, rest = refs[:size], refs[size:]
    gain_ref, wq_ref, wk_ref, wv_ref = rest[:4]
    out_refs, scratch = rest[4:-4], rest[-4:]
    rows_ref = scratch[0]
    slot, head = pl.program_id(0), pl.program_id(1)
    block, width = out_refs[0].shape[1:]
    tile = in_refs[0].shape[1]
    tiles = block // tile
    gain = gain_ref[0].astype(F32)
    for k, ref in enumerate(in_refs):
        start = pl.multiple_of((me[0] ^ k) * block, block)
        rows = ref[pl.ds(head * tiles, tiles)].reshape(block, width)
        out_refs[k][1] = rows
        packed = ref[ref.shape[0] - 1].astype(F32)
        scale = jnp.concatenate(
            [
                packed[:, 4 * t : 4 * t + 1]
                + packed[:, 4 * t + 1 : 4 * t + 2]
                + packed[:, 4 * t + 2 : 4 * t + 3]
                for t in range(tiles)
            ],
            axis=0,
        )
        rows_ref[pl.ds(start, block), :] = (rows.astype(F32) * scale * gain).astype(BF)
    base = which[slot] * (ids.shape[0] // 2)
    mixed = attend(wq_ref[...], wk_ref[...], wv_ref[...], *scratch, block, ids, base)
    rows_ref[...] = mixed
    for k, out_ref in enumerate(out_refs):
        start = pl.multiple_of((me[0] ^ k) * block, block)
        out_ref[0] = rows_ref[pl.ds(start, block), :]


def attention_send(which, me, ids, blocks, gain, wq, wk, wv):
    size = len(blocks)
    slots = blocks[0].shape[0]
    heads, width = wq.shape[1], wq.shape[2]
    weight_spec = pl.BlockSpec(
        (None, None, width, width), lambda k, h, which, me, ids: (which[k], h, 0, 0)
    )
    block_spec = pl.BlockSpec(
        (None, *blocks[0].shape[1:]), lambda k, h, which, me, ids: (k, 0, 0, 0)
    )
    return pl.pallas_call(
        attention_send_kernel,
        out_shape=[jax.ShapeDtypeStruct((slots, 2, heads, BLK, width), BF)] * size,
        grid_spec=pltpu.PrefetchScalarGridSpec(
            num_scalar_prefetch=3,
            grid=(slots, heads),
            in_specs=[block_spec] * size
            + [
                pl.BlockSpec(
                    (1, 1, width),
                    lambda k, h, which, me, ids: (which[k], 0, me[0] * heads + h),
                ),
                weight_spec,
                weight_spec,
                weight_spec,
            ],
            out_specs=[
                pl.BlockSpec(
                    (None, 2, None, BLK, width), lambda k, h, which, me, ids: (k, 0, h, 0, 0)
                )
            ]
            * size,
            scratch_shapes=attention_scratch(size * BLK, width),
        ),
        cost_estimate=attention_cost(slots, heads, size, BLK, width),
        name="attention_send",
    )(which, me, ids, *blocks, gain, wq, wk, wv)


def mix_final_kernel(which, me, target, *refs):
    in_refs, (w_ref, out_ref, wide_ref, state_ref) = refs[:-4], refs[-4:]
    heads = wide_ref.shape[0]
    width = wide_ref.shape[2]
    per = in_refs[0].shape[1]
    for k, in_ref in enumerate(in_refs):
        group = me[0] ^ k
        for h in range(per):
            wide_ref[group * per + h] = in_ref[0, h].astype(F32)
            state_ref[group * per + h] = in_ref[1, h]
    step = 4

    def body(i, carry):
        totals = mix_totals(wide_ref, w_ref, i, step)
        for k in range(step):
            g = i * step + k
            lanes = pl.ds(pl.multiple_of(g * width, width), width)
            out_ref[:, lanes] = (state_ref[g].astype(F32) + totals[k]).astype(BF)
        return carry

    lax.fori_loop(0, heads // step, body, 0)


def mix_final(which, me, target, blocks, weights):
    size = len(blocks)
    slots, _, per, rows, width = blocks[0].shape
    heads = size * per
    pairs = weights.shape[1]
    return pl.pallas_call(
        mix_final_kernel,
        out_shape=jax.ShapeDtypeStruct((slots, rows, heads * width), BF),
        grid_spec=pltpu.PrefetchScalarGridSpec(
            num_scalar_prefetch=3,
            grid=(slots,),
            in_specs=[
                pl.BlockSpec(
                    (None, *blocks[0].shape[1:]), lambda k, which, me, target: (k, 0, 0, 0, 0)
                )
            ]
            * size
            + [pl.BlockSpec((1, pairs, width), lambda k, which, me, target: (which[k], 0, 0))],
            out_specs=pl.BlockSpec(
                (None, rows, heads * width), lambda k, which, me, target: (target[k], 0, 0)
            ),
            scratch_shapes=[
                pltpu.VMEM((heads, rows, width), F32),
                pltpu.VMEM((heads, rows, width), BF),
            ],
        ),
        cost_estimate=mix_cost(slots, rows, heads * width, pairs, width),
        name="mix_final",
    )(which, me, target, *blocks, weights)


def exchange(value):
    return lax.all_to_all(value, "fsdp", split_axis=0, concat_axis=0, tiled=True)


def send_on(blocks):
    segments, size = lax.axis_size("segment"), lax.axis_size("fsdp")
    arrived = []
    for k, block in enumerate(blocks):
        pairs = []
        for s in range(segments):
            for f in range(size):
                pairs.append((s * size + f, (s + 1) % segments * size + (f ^ k)))
        arrived.append(lax.ppermute(block, ("segment", "fsdp"), pairs))
    return arrived


def shifted(value):
    devices = lax.axis_size("segment")
    return lax.ppermute(value, "segment", [(i, (i + 1) % devices) for i in range(devices)])


def tie(value, *others):
    return lax.optimization_barrier((value, *others))[0]


def shards(stream, gain, w_query, w_key, w_value, w_mix, active, random_blocks):
    segments = lax.axis_size("segment")
    segment = lax.axis_index("segment")
    size = lax.axis_size("fsdp")
    slots = stream.shape[0]
    me = lax.axis_index("fsdp").astype(jnp.int32).reshape(1)
    wq, wk, wv = w_query[:, 0], w_key[:, 0], w_value[:, 0]
    ids = random_blocks[:, 0].reshape(-1)
    whole = stream[:, 0]

    def layers_of(place, turn):
        turned = jnp.where(place < turn, 1, 0)
        return ((jnp.arange(slots, dtype=jnp.int32) + turned) % slots).astype(jnp.int32)

    first = layers_of(segment, 0)
    second = layers_of(segment, 1)
    mixing = layers_of((segment + segments - 1) % segments, 1)
    target = layers_of(segment, 2)

    live = (active[:, 0] > 0)[:, None, None, None]
    masked = jnp.where(live, w_mix[:, 0], jnp.zeros_like(w_mix[:, 0]))
    masked = masked.reshape(1, slots, masked.shape[1], -1)
    bits = [1 << b for b in reversed(range(size.bit_length() - 1))]
    place = gathered_place(bits)

    own = partner(masked, bits[0])
    normed = norm(first, whole, gain, size)
    rows = exchange(tie(normed, own))
    own = partner(own, bits[1])
    left = shifted(tie(masked, normed))
    rows = tie(rows, own, left)
    own = partner(tie(own, rows), bits[2])
    left = partner(tie(left, rows), bits[0])
    attended = attention(first, ids, rows, wq, wk, wv)
    back = exchange(tie(attended, own, left))
    own = mix_weights(place, own)
    left = partner(left, bits[1])
    back = tie(back, left, own)
    here = send_on(mix_send(first, me, back, own, whole))
    left = partner(tie(left, *here), bits[2])
    attended = attention_send(second, me, ids, here, gain, wq, wk, wv)
    *attended, left = lax.optimization_barrier((*attended, left))
    last = send_on(attended)
    left = mix_weights(place, left)
    done = mix_final(mixing, me, target, last, left)
    return done[:, None]


def solution(mesh):
    in_specs = (
        P(None, "segment", "fsdp", None),
        P(None, "segment", None),
        P(None, "segment", "fsdp", None, None),
        P(None, "segment", "fsdp", None, None),
        P(None, "segment", "fsdp", None, None),
        P(None, "segment", "fsdp", None, None),
        P(None, "segment"),
        P(None, "segment", None, None),
    )
    out_specs = P(None, "segment", "fsdp", None)
    return jax.shard_map(shards, mesh=mesh, in_specs=in_specs, out_specs=out_specs, check_vma=False)
```
